256 devices in a mesh: chan: 32 (over y, z), bins: 8 (over x, core).
Axes of the slice: x: 4, y: 4, z: 8, core: 2. Of those that a mesh axis runs over, the one named last changes fastest.
Arguments:
- effects: bfloat16 [256, 16384, 256], P('chan', 'bins'), may hold values from -0.19921875 to 0.19921875
- nominal: float32 [256, 16384], P('chan', 'bins'), may hold values from 0.2 to 5
- observed: int32 [256, 16384], P('chan', 'bins'), may hold values from 0 to 7
- mc_variance: float32 [256, 16384], P('chan', 'bins'), may hold values from 0.002 to 0.5
- theta: float32 [8192], replicated, may hold values from -4 to 4
- nuisance_index: int32 [256, 256], replicated, may hold values from 0 to 8191, as said below
- bin_counts: int32 [256], P('chan'), may hold values from 1 to 16384, 2097152 in all
- tile_owner: int32 [256], replicated, may hold values from 0 to 255, each once
Outputs:
- hessian_tiles: float32 [256, 512, 512], P(('chan', 'bins'))
- gradient: float32 [8192], P(('chan', 'bins'))
The draws below stay inside these ranges and needn't reach their ends.
Inputs may be any that keep to these rules, and one draw needn't show every extreme that they name: `nuisance_index`: each channel's list is 2 runs of 128 consecutive nuisances, each run starting at a multiple of 128, the runs distinct and in increasing order. Bins at positions bin_counts[c] and beyond of channel c carry no data. `tile_owner`: every tile number appears exactly once.
All inputs are finite; a program needn't handle non-finite values. No bound on the sum of `bin_counts` on one device may be relied on, other than what follows from the above.
Results may differ from the reference program's by a relative error of at most 0.0029.
Values sent between devices are 32-bit elements; how exact they have to be, the bound alone decides.
No kernel may reach another device: no remote copies, remote signals or barrier semaphores. Data moves between devices by JAX's collectives and lax.ppermute only.
A program may use at most 128 MiB of HBM per device.

```python
import math
import jax
import jax.numpy as jnp
import numpy as np
from jax import lax

NU = 8192
K = 256
GW = 128
TILE = 512
CH = 256
BC = 16384
NTS = 16
NT = 256


def draw_nuisance_index(key, part):
    group_count = NU // GW
    group_parts = K // GW
    channel_keys = jax.random.split(jax.random.fold_in(key, 17), CH)

    def one_channel(channel_key):
        shuffled = jax.random.permutation(channel_key, group_count)
        picked = jnp.sort(shuffled[:group_parts])
        return (picked[:, None] * GW + jnp.arange(GW)[None, :]).reshape(-1)
    return jax.vmap(one_channel)(channel_keys).astype(jnp.int32)


def with_ends(values, rng, least, top_value):
    dims = values.shape
    place = [jax.random.randint(jax.random.fold_in(rng, axis), (), 0, dims[axis]) for axis in range(len(dims))]
    values = values.at[tuple(place)].set(least)
    longest = dims.index(max(dims))
    place[longest] = (place[longest] + 1) % dims[longest]
    return values.at[tuple(place)].set(top_value)


def levels(stream_key, extent, shards, least, largest):
    factor_of = 1.0
    for position, shards_of in shards:
        steps = jax.random.uniform(jax.random.fold_in(jax.random.fold_in(stream_key, 6), position), (shards_of,), jnp.float32, least / len(shards), largest / len(shards))
        factor_of = factor_of * jnp.repeat(jnp.exp(steps), extent[position] // shards_of).reshape((-1,) + (1,) * (len(extent) - 1 - position))
    return factor_of


def split_up(amount, total, most, slope):
    loads = [(1 << 20) // math.isqrt(grade ** slope) + 1 for grade in range(2, amount + 1)]
    surplus, given = total - most - (amount - 1), [1] * (amount - 1)
    while surplus > 0:
        candidates = [i for i in range(amount - 1) if given[i] < most]
        whole, remaining = sum([loads[i] for i in candidates]), surplus
        for i in candidates:
            extra = min(most - given[i], max(1, remaining * loads[i] // whole), surplus)
            given[i] = given[i] + extra
            surplus = surplus - extra
    return np.array([most] + given)


def ragged_sizes(rng, number_of, total, limit, lean):
    if number_of == 2:
        one = jax.random.randint(rng, (), max(1, total - limit), min(limit, total - 1) + 1)
        return jnp.stack([one, total - one])
    tallies = jnp.asarray(split_up(number_of, total, limit, lean), jnp.int32)
    pairs = (number_of - 1) // 2
    giver, receiver = tallies[1:1 + 2 * pairs:2], tallies[2:2 + 2 * pairs:2]
    margin = jnp.minimum(giver - 1, limit - receiver)
    moved = jax.random.randint(jax.random.fold_in(rng, 1), (pairs,), 0, 1 << 20) % (margin + 1)
    tallies = tallies.at[1:1 + 2 * pairs:2].set(giver - moved).at[2:2 + 2 * pairs:2].set(receiver + moved)
    return tallies[jax.random.permutation(jax.random.fold_in(rng, 2), number_of)]


def gaussian(own_key, extent, spread, most, cuts=(), kind=jnp.bfloat16):
    level = levels(own_key, extent, cuts, -0.22, 0.18) if cuts else 1.0
    result = jax.random.normal(own_key, extent, jnp.float32) * spread * level
    return jnp.minimum(jnp.maximum(result, -most), most).astype(kind)


def setup_inputs(seed: int = 0) -> dict:
    arg_keys = jax.random.split(jax.random.key(seed), 9)
    return {
        "effects": gaussian(arg_keys[0], (CH, BC, K), 0.04, 0.19921875, ((0, 32), (1, 8))),
        "nominal": jnp.clip(jnp.exp(math.log(5.0) - 3.218876 * jax.random.uniform(arg_keys[1], (CH, BC), jnp.float32) ** levels(arg_keys[1], (CH, BC), ((0, 32), (1, 8)), -0.2, 0.2)), 0.2, 5.0),
        "observed": with_ends(jax.random.randint(arg_keys[2], (CH, BC), 0, 8), jax.random.fold_in(arg_keys[2], 1), 0, 7).astype(jnp.int32),
        "mc_variance": jnp.clip(jnp.exp(math.log(0.5) - 5.521461 * jax.random.uniform(arg_keys[3], (CH, BC), jnp.float32) ** levels(arg_keys[3], (CH, BC), ((0, 32), (1, 8)), -0.2, 0.2)), 0.002, 0.5),
        "theta": gaussian(arg_keys[4], (NU,), 1.0, 4.0, (), jnp.float32),
        "nuisance_index": draw_nuisance_index(jax.random.fold_in(arg_keys[8], 71), 0),
        "bin_counts": ragged_sizes(arg_keys[6], CH, CH * BC // 2, BC, 2).astype(jnp.int32),
        "tile_owner": jax.random.permutation(arg_keys[7], NT).astype(jnp.int32),
    }


def reference(effects, nominal, observed, mc_variance, theta, nuisance_index, bin_counts, tile_owner):
    positions = jnp.arange(BC, dtype=jnp.int32)

    def channel_step(carry, inputs):
        hessian, gradient = carry
        matrix, nominal_row, observed_row, variance_row, indices, used = inputs
        chosen = theta[indices].astype(jnp.bfloat16)
        exponent = jnp.dot(matrix, chosen, preferred_element_type=jnp.float32)
        expected = nominal_row * jnp.exp(exponent)
        denominator = 1.0 + expected * variance_row
        live = positions < used
        residual = jnp.where(live, (expected - observed_row) / denominator, 0.0)
        weight = jnp.where(live, expected / denominator, 0.0)
        scaled = (jnp.sqrt(weight)[:, None] * matrix).astype(jnp.bfloat16)
        block = jnp.dot(scaled.T, scaled, preferred_element_type=jnp.float32)
        gradient_part = jnp.dot(residual.astype(jnp.bfloat16), matrix, preferred_element_type=jnp.float32)
        hessian = hessian.at[indices[:, None], indices[None, :]].add(block)
        gradient = gradient.at[indices].add(gradient_part)
        return ((hessian, gradient), None)
    initial = (jnp.zeros((NU, NU), jnp.float32), jnp.zeros((NU,), jnp.float32))
    totals, ignored = lax.scan(channel_step, initial, (effects, nominal, observed, mc_variance, nuisance_index, bin_counts))
    hessian = totals[0] + jnp.eye(NU, dtype=jnp.float32)
    tiles = hessian.reshape(NTS, TILE, NTS, TILE).transpose(0, 2, 1, 3).reshape(NT, TILE, TILE)
    return (tiles[tile_owner], totals[1] + theta)
```

```python
import jax
import jax.numpy as jnp
from jax import lax
from jax.experimental import pallas as pl
from jax.experimental.pallas import tpu as pltpu
from jax.sharding import PartitionSpec as P

GW = 128
TILE = 512
NY, NZ, NX, NC = 4, 8, 4, 2
QA, QB = 18, 17
GROUP_A, GROUP_B = 4, 8
F32, BF16 = jnp.float32, jnp.bfloat16


def z_shift(s):
    return [(y * NZ + z, y * NZ + (z + s) % NZ) for y in range(NY) for z in range(NZ)]


def y_shift(s):
    return [(y * NZ + z, (y + s) % NY * NZ + z) for y in range(NY) for z in range(NZ)]


def x_shift(s, flip):
    return [(x * NC + c, (x + s) % NX * NC + (c ^ flip)) for x in range(NX) for c in range(NC)]


def on_chan(value, perm):
    return lax.ppermute(value, "chan", perm)


def joined(parts):
    return parts[0] if len(parts) == 1 else jnp.concatenate(parts, axis=0)


def z_ring(pieces):
    count = len(pieces)
    found = {0: list(pieces)}
    up, down = list(pieces), list(pieces)
    for s in (1, 2, 3):
        up = [on_chan(v, z_shift(1)) for v in up]
        down = [on_chan(v, z_shift(-1)) for v in down]
        found[s], found[NZ - s] = up, down
    half = (count + 1) // 2
    found[4] = [
        on_chan(up[k], z_shift(1)) if k < half else on_chan(down[k], z_shift(-1)) for k in range(count)
    ]
    return found


def y_ring(pieces):
    count = len(pieces)
    up = [on_chan(v, y_shift(1)) for v in pieces]
    down = [on_chan(v, y_shift(-1)) for v in pieces]
    half = (count + 1) // 2
    far = [
        on_chan(up[k], y_shift(1)) if k < half else on_chan(down[k], y_shift(-1)) for k in range(count)
    ]
    return {0: list(pieces), 1: up, 2: far, 3: down}


def gather_a(own):
    first = [own] + [on_chan(own, y_shift(d)) for d in (1, 2, 3)]
    pieces = [joined(first[k : k + GROUP_A]) for k in range(0, NY, GROUP_A)]
    found = z_ring(pieces)
    where = {
        (dy, dz): (found[dz][dy // GROUP_A], dy % GROUP_A * QA) for dy in range(NY) for dz in range(NZ)
    }
    return where


def gather_b(own):
    around = z_ring([own])
    first = [around[d][0] for d in range(NZ)]
    pieces = [joined(first[k : k + GROUP_B]) for k in range(0, NZ, GROUP_B)]
    found = y_ring(pieces)
    where = {
        (dy, dz): (found[dy][dz // GROUP_B], dz % GROUP_B * QB) for dy in range(NY) for dz in range(NZ)
    }
    return where


def pack_kernel(place_ref, blocks_ref, grad_ref, mine_ref, other_ref, a_ref, o_ref, b_ref):
    x, core = place_ref[0], place_ref[1]
    for c in range(8):
        rows = slice(c * GW, (c + 1) * GW)
        a_ref[rows] = blocks_ref[c * 256 : c * 256 + GW, :GW]
        o_ref[rows] = blocks_ref[c * 256 : c * 256 + GW, GW:]
        b_ref[rows] = blocks_ref[c * 256 + GW : c * 256 + 256, GW:]
    lane = lax.broadcasted_iota(jnp.int32, (8, GW), 1)
    diag = jnp.zeros((8, GW), F32)
    for row in range(GW):
        a = a_ref[pl.ds(row, 8, stride=GW), :]
        diag = jnp.where(lane == row, a, diag)
    grads = grad_ref[...]
    for d in range(NX):
        for ref, side in ((mine_ref, core), (other_ref, 1 - core)):
            start = lax.rem(x + d, NX) * 32 + side * 16
            for q in range(16):
                row = start + q
                ref[d, q] = o_ref[pl.ds(row, 8, stride=GW), :]
                a = a_ref[pl.ds(row, 8, stride=GW), :]
                b = b_ref[pl.ds(row, 8, stride=GW), :]
                ref[d, QA + q] = jnp.where(lane > row, a, b)
            ref[d, 16] = grads[:, :GW]
            ref[d, 17] = grads[:, GW:]
            ref[d, QA + 16] = diag


def split2(v):
    high = v.astype(BF16)
    return high, (v - high.astype(F32)).astype(BF16)


def place_kernel(arrays, offsets_a, offsets_b, place_ref, meta_ref, *refs):
    ins, (mine_ref, other_ref, grad_ref) = refs[:arrays], refs[arrays:]
    core, slice_index, x = place_ref[1], place_ref[2], place_ref[0]
    pos = lax.broadcasted_iota(jnp.int32, (128, 256), 0)
    meta = meta_ref[...]

    def hot(*rows):
        hit = pos == meta[rows[0] : rows[0] + 1]
        for r in rows[1:]:
            hit = jnp.logical_or(hit, pos == meta[r : r + 1])
        return jnp.where(hit, 1.0, 0.0).astype(BF16)

    sel_off = hot(0, 1)
    sel_both = jnp.concatenate([hot(2), hot(3)], axis=0)
    lane = lax.broadcasted_iota(jnp.int32, (128, GW), 1)

    def gathered(offsets, q):
        return jnp.concatenate([ins[k][o + q] for k, o in offsets], axis=0)

    def apply(sel, v):
        high, low = split2(v)
        return jnp.dot(sel, high, preferred_element_type=F32) + jnp.dot(
            sel, low, preferred_element_type=F32
        )

    diag = apply(sel_both[:128], gathered(offsets_b, 16))
    grads = apply(hot(4)[:8], gathered(offsets_a, 16)) + apply(hot(5)[:8], gathered(offsets_a, 17))
    grad_ref[...] = grads
    for q in range(0, 16, 2):
        off = apply(
            sel_off, jnp.concatenate([gathered(offsets_a, q), gathered(offsets_a, q + 1)], axis=1)
        )
        both = apply(
            sel_both, jnp.concatenate([gathered(offsets_b, q), gathered(offsets_b, q + 1)], axis=1)
        )
        for k in range(2):
            row = slice_index * 16 + q + k
            cols = slice(k * GW, (k + 1) * GW)
            upper, lower = both[:128, cols], both[128:, cols]
            value = off[:, cols] + jnp.where(lane > row, upper, lower)
            value = value + jnp.where(lane == row, diag, 0.0)
            value = value.reshape(NX, NC, 16, GW)
            del upper, lower
            for d in range(NX):
                mine_ref[d, q + k] = value[d, 0]
                other_ref[d, q + k] = value[d, 1]


def finish_kernel(place_ref, *refs):
    ins, out_ref, tile_ref = refs[:8], refs[8], refs[9]
    x, core, tile_row, tile_col = place_ref[0], place_ref[1], place_ref[3], place_ref[4]
    k = 0
    for flip in range(NC):
        for d in range(NX):
            source = lax.rem(x - d + NX, NX) * 2 + (core + flip) % 2
            for rc in range(16):
                start = pl.multiple_of(source * 16 + rc // 4 * GW, 16)
                tile_ref[pl.ds(start, 16), rc % 4 * GW : (rc % 4 + 1) * GW] = ins[k][
                    pl.ds(rc, 16, stride=16), :
                ]
            k += 1

    @pl.when(tile_row < tile_col)
    def _():
        out_ref[0] = tile_ref[...]

    @pl.when(tile_row > tile_col)
    def _():
        for r in range(4):
            for c in range(4):
                out_ref[0, r * GW : (r + 1) * GW, c * GW : (c + 1) * GW] = tile_ref[
                    c * GW : (c + 1) * GW, r * GW : (r + 1) * GW
                ].T

    @pl.when(tile_row == tile_col)
    def _():
        row = lax.broadcasted_iota(jnp.int32, (GW, GW), 0)
        col = lax.broadcasted_iota(jnp.int32, (GW, GW), 1)
        for r in range(4):
            for c in range(4):
                here = tile_ref[r * GW : (r + 1) * GW, c * GW : (c + 1) * GW]
                there = tile_ref[c * GW : (c + 1) * GW, r * GW : (r + 1) * GW].T
                value = here + there
                if r == c:
                    value = jnp.where(row == col, here + 1.0, value)
                out_ref[0, r * GW : (r + 1) * GW, c * GW : (c + 1) * GW] = value


VMEM = pl.BlockSpec(memory_space=pltpu.VMEM)
SMEM = pl.BlockSpec(memory_space=pltpu.SMEM)


def shape(*dims):
    return jax.ShapeDtypeStruct(dims, F32)


def cost(flops, moved):
    return pl.CostEstimate(flops=flops, bytes_accessed=moved, transcendentals=0)


def local(effects, nominal, observed, mc_variance, theta, nuisance_index, bin_counts, tile_owner):
    chan_index, bins_index = lax.axis_index("chan"), lax.axis_index("bins")
    y, z, x, core = chan_index // NZ, chan_index % NZ, bins_index // NC, bins_index % NC
    chans, bins, width = effects.shape
    tile_side = theta.shape[0] // TILE
    groups = nuisance_index[:, ::GW] // GW
    own_groups = lax.dynamic_slice_in_dim(groups, chan_index * chans, chans, 0)
    chosen = theta.reshape(-1, GW)[own_groups].reshape(chans, width).astype(BF16)
    slot = chan_index * (NX * NC) + bins_index
    own_tile = lax.dynamic_slice_in_dim(tile_owner, slot, 1, 0)[0]
    place = jnp.stack([x, core, bins_index, own_tile // tile_side, own_tile % tile_side]).astype(jnp.int32)

    exponent = jnp.einsum("cbk,ck->cb", effects, chosen, preferred_element_type=F32)
    expected = nominal * jnp.exp(exponent)
    denominator = 1.0 + expected * mc_variance
    positions = bins_index * bins + lax.broadcasted_iota(jnp.int32, (chans, bins), 1)
    live = positions < bin_counts[:, None]
    residual = jnp.where(live, (expected - observed) / denominator, 0.0)
    weight = jnp.where(live, expected / denominator, 0.0)
    scaled = (jnp.sqrt(weight)[:, :, None] * effects).astype(BF16)
    grads = jnp.einsum("cbk,cb->ck", effects, residual.astype(BF16), preferred_element_type=F32)
    blocks = jnp.einsum("cbk,cbl->ckl", scaled, scaled, preferred_element_type=F32)

    tiles = QA + QB
    mine, other = pl.pallas_call(
        pack_kernel,
        out_shape=[shape(NX, tiles, 8, GW)] * 2,
        in_specs=[SMEM, VMEM, VMEM],
        out_specs=[VMEM] * 2,
        scratch_shapes=[pltpu.VMEM((8 * GW, GW), F32)] * 3,
        cost_estimate=cost(10**6, 4 * 10**6),
        name="pack",
    )(place, blocks.reshape(chans * width, width), grads)
    other = lax.ppermute(other, "bins", x_shift(0, 1))
    chip = [mine[d] + other[d] for d in range(NX)]
    arrived = [lax.ppermute(chip[d], "bins", x_shift(d, 0)) for d in (1, 2, 3)]
    own_a = chip[0][:QA] + arrived[0][:QA] + arrived[1][:QA] + arrived[2][:QA]
    own_b = chip[0][QA:] + arrived[0][QA:] + arrived[1][QA:] + arrived[2][QA:]

    at_a, at_b = gather_a(own_a), gather_b(own_b)
    order = [(dy, dz) for dy in range(NY) for dz in range(NZ)]
    arrays, offsets_a, offsets_b = [], [], []
    for at, offsets in ((at_a, offsets_a), (at_b, offsets_b)):
        for key in order:
            array, offset = at[key]
            known = [k for k, v in enumerate(arrays) if v is array]
            if not known:
                arrays.append(array)
                known = [len(arrays) - 1]
            offsets.append((known[0], offset))

    dy = jnp.arange(NY, dtype=jnp.int32)[:, None, None]
    dz = jnp.arange(NZ, dtype=jnp.int32)[None, :, None]
    channel = ((y - dy + NY) % NY * NZ + (z - dz + NZ) % NZ) * chans
    channel = (channel + jnp.arange(chans, dtype=jnp.int32)).reshape(-1)
    first, second = groups[channel, 0], groups[channel, 1]
    rel_x = jnp.arange(NX, dtype=jnp.int32)
    row_tiles = lax.dynamic_slice_in_dim(tile_owner, chan_index * 8, 8, 0)
    rel = (jnp.arange(8, dtype=jnp.int32) // NC - x + NX) % NX * NC + (jnp.arange(8, dtype=jnp.int32) + core) % NC
    per = TILE // GW

    def slot_of(tile_ids, inside):
        hit = row_tiles[:, None] == tile_ids[None, :]
        base = jnp.sum(jnp.where(hit, rel[:, None] * 16 + inside[None, :] + 1, 0), axis=0)
        return base - 1

    tr, tc = first // per, second // per
    inside = first % per * per + second % per
    straight = slot_of(tr * tile_side + tc, inside)
    mirrored = jnp.where(tr == tc, -1, slot_of(tc * tile_side + tr, inside))
    upper = slot_of(tr * (tile_side + 1), first % per * (per + 1))
    lower = slot_of(tc * (tile_side + 1), second % per * (per + 1))
    meta = jnp.stack(
        [straight, mirrored, upper, lower, first - 2 * chan_index, second - 2 * chan_index, upper, lower]
    )
    del rel_x

    import functools

    mine, other, grad_rows = pl.pallas_call(
        functools.partial(place_kernel, len(arrays), offsets_a, offsets_b),
        out_shape=[shape(NX, 16, 16, GW)] * 2 + [shape(8, GW)],
        in_specs=[SMEM, VMEM] + [VMEM] * len(arrays),
        out_specs=[VMEM] * 3,
        cost_estimate=cost(10**9, 6 * 10**6),
        name="place",
    )(place, meta, *arrays)

    ins = [mine[0]] + [lax.ppermute(mine[d], "bins", x_shift(d, 0)) for d in (1, 2, 3)]
    ins += [lax.ppermute(other[d], "bins", x_shift(d, 1)) for d in range(NX)]
    hessian_tiles = pl.pallas_call(
        finish_kernel,
        out_shape=shape(1, TILE, TILE),
        in_specs=[SMEM] + [VMEM] * 8,
        out_specs=VMEM,
        scratch_shapes=[pltpu.VMEM((TILE, TILE), F32)],
        cost_estimate=cost(10**6, 2 * 10**6),
        name="finish",
    )(place, *[v.reshape(256, GW) for v in ins])

    part = lax.dynamic_slice(
        grad_rows, (bins_index // 4, bins_index % 4 * 32), (1, 32)
    ).reshape(-1)
    gradient = part + lax.dynamic_slice_in_dim(theta, slot * 32, 32, 0)
    return hessian_tiles, gradient


def solution(mesh):
    return jax.shard_map(
        local,
        mesh=mesh,
        in_specs=(
            P("chan", "bins", None),
            P("chan", "bins"),
            P("chan", "bins"),
            P("chan", "bins"),
            P(),
            P(),
            P("chan"),
            P(),
        ),
        out_specs=(P(("chan", "bins"), None, None), P(("chan", "bins"))),
        check_vma=False,
    )
```

```python
import functools

import jax
import jax.numpy as jnp
from jax import lax
from jax.experimental import pallas as pl
from jax.experimental.pallas import tpu as pltpu
from jax.sharding import PartitionSpec as P

GW = 128
TILE = 512
NY, NZ, NX, NC = 4, 8, 4, 2
QA, QB = 18, 17
F32, BF16 = jnp.float32, jnp.bfloat16


def z_shift(s):
    return [(y * NZ + z, y * NZ + (z + s) % NZ) for y in range(NY) for z in range(NZ)]


def y_shift(s):
    return [(y * NZ + z, (y + s) % NY * NZ + z) for y in range(NY) for z in range(NZ)]


def x_shift(s, flip):
    return [(x * NC + c, (x + s) % NX * NC + (c ^ flip)) for x in range(NX) for c in range(NC)]


def on_chan(value, perm):
    return lax.ppermute(value, "chan", perm)


def gather_a(own):
    near = [own] + [on_chan(own, y_shift(d)) for d in (1, 2, 3)]
    held = jnp.concatenate(near, axis=0)
    up, down = held, held
    found = {0: held}
    for s in (1, 2, 3):
        up, down = on_chan(up, z_shift(1)), on_chan(down, z_shift(-1))
        found[s], found[NZ - s] = up, down
    half = NY // 2
    far = (on_chan(up[: half * QA], z_shift(1)), on_chan(down[half * QA :], z_shift(-1)))
    where = {(dy, dz): (found[dz], dy * QA) for dy in range(NY) for dz in range(NZ) if dz != 4}
    where.update({(dy, 4): (far[dy // half], dy % half * QA) for dy in range(NY)})
    return where


def gather_b(own):
    near = {0: own}
    for d in (1, 2, -2, -1):
        near[d % NZ] = on_chan(own, z_shift(d))
    near[3] = on_chan(near[2], z_shift(1))
    near[4] = on_chan(near[2], z_shift(2))
    near[5] = on_chan(near[6], z_shift(-1))
    held = jnp.concatenate([near[d] for d in range(NZ)], axis=0)
    up, down = on_chan(held, y_shift(1)), on_chan(held, y_shift(-1))
    half = NZ // 2
    far = (on_chan(up[: half * QB], y_shift(1)), on_chan(down[half * QB :], y_shift(-1)))
    found = {0: held, 1: up, 3: down}
    where = {(dy, dz): (found[dy], dz * QB) for dy in (0, 1, 3) for dz in range(NZ)}
    where.update({(2, dz): (far[dz // half], dz % half * QB) for dz in range(NZ)})
    return where


def here(device):
    bins_index = lax.rem(device, NX * NC)
    return lax.div(bins_index, NC), lax.rem(bins_index, NC), bins_index


def bins_kernel(
    device_ref, index_ref, counts_ref, theta_ref, nominal_ref, observed_ref, variance_ref, effects_ref,
    mine_ref, other_ref, a_ref, o_ref, b_ref, g_ref,
):
    c = pl.program_id(0)
    x, core, bins_index = here(device_ref[0])
    count = effects_ref.shape[1]
    effects = effects_ref[0]
    chosen = jnp.concatenate(
        [theta_ref[pl.ds(lax.div(index_ref[c, k * GW], GW), 1), :] for k in range(2)], axis=1
    )
    chosen = jnp.broadcast_to(chosen, (8, 2 * GW)).astype(BF16)
    exponent = lax.dot_general(chosen, effects, (((1,), (1,)), ((), ())), preferred_element_type=F32)[:1]
    expected = nominal_ref[pl.ds(c, 1), :] * jnp.exp(exponent)
    denominator = 1.0 + expected * variance_ref[pl.ds(c, 1), :]
    positions = bins_index * count + lax.broadcasted_iota(jnp.int32, (1, count), 1)
    live = positions < counts_ref[c]
    residual = jnp.where(
        live, (expected - observed_ref[pl.ds(c, 1), :].astype(F32)) / denominator, 0.0
    )
    root = jnp.sqrt(jnp.where(live, expected / denominator, 0.0))
    g_ref[pl.ds(c, 1), :] = jnp.dot(
        jnp.broadcast_to(residual, (8, count)).astype(BF16), effects, preferred_element_type=F32
    )[:1]
    column = jnp.broadcast_to(root, (GW, count)).T
    scaled = (jnp.concatenate([column, column], axis=1) * effects.astype(F32)).astype(BF16)
    left, right = scaled[:, :GW], scaled[:, GW:]

    both = lax.dot_general(left, scaled, (((0,), (0,)), ((), ())), preferred_element_type=F32)
    rows = pl.ds(pl.multiple_of(c * GW, GW), GW)
    a_ref[rows, :] = both[:, :GW]
    o_ref[rows, :] = both[:, GW:]
    b_ref[rows, :] = lax.dot_general(right, right, (((0,), (0,)), ((), ())), preferred_element_type=F32)

    @pl.when(c == pl.num_programs(0) - 1)
    def _():
        lane = lax.broadcasted_iota(jnp.int32, (8, GW), 1)
        diag = jnp.zeros((8, GW), F32)
        for row in range(GW):
            diag = jnp.where(lane == row, a_ref[pl.ds(row, 8, stride=GW), :], diag)
        grads = g_ref[...]
        for d in range(NX):
            for ref, side in ((mine_ref, core), (other_ref, 1 - core)):
                start = lax.rem(x + d, NX) * 32 + side * 16
                for q in range(16):
                    row = start + q
                    ref[d, q] = o_ref[pl.ds(row, 8, stride=GW), :]
                    a = a_ref[pl.ds(row, 8, stride=GW), :]
                    b = b_ref[pl.ds(row, 8, stride=GW), :]
                    ref[d, QA + q] = jnp.where(lane > row, a, b)
                ref[d, 16] = grads[:, :GW]
                ref[d, 17] = grads[:, GW:]
                ref[d, QA + 16] = diag


def split2(v):
    high = v.astype(BF16)
    return high, (v - high.astype(F32)).astype(BF16)


def place_kernel(arrays, offsets_a, offsets_b, device_ref, meta_ref, *refs):
    ins, outs, grad_ref = refs[:arrays], refs[arrays:-1], refs[-1]
    slice_index = here(device_ref[0])[2]
    pos = lax.broadcasted_iota(jnp.int32, (128, 256), 0)
    meta = meta_ref[...]

    def hot(*rows):
        hit = pos == meta[rows[0] : rows[0] + 1]
        for r in rows[1:]:
            hit = jnp.logical_or(hit, pos == meta[r : r + 1])
        return jnp.where(hit, 1.0, 0.0).astype(BF16)

    sel_off = hot(0, 1)
    sel_both = jnp.concatenate([hot(2), hot(3)], axis=0)
    lane = lax.broadcasted_iota(jnp.int32, (128, GW), 1)

    def gathered(offsets, q):
        return jnp.concatenate([ins[k][o + q] for k, o in offsets], axis=0)

    def apply(sel, v):
        high, low = split2(v)
        return jnp.dot(sel, high, preferred_element_type=F32) + jnp.dot(
            sel, low, preferred_element_type=F32
        )

    diag = apply(sel_both[:128], gathered(offsets_b, 16))
    grads = apply(hot(4)[:8], gathered(offsets_a, 16)) + apply(hot(5)[:8], gathered(offsets_a, 17))
    grad_ref[...] = grads
    for q in range(0, 16, 2):
        off = apply(
            sel_off, jnp.concatenate([gathered(offsets_a, q), gathered(offsets_a, q + 1)], axis=1)
        )
        both = apply(
            sel_both, jnp.concatenate([gathered(offsets_b, q), gathered(offsets_b, q + 1)], axis=1)
        )
        for k in range(2):
            row = slice_index * 16 + q + k
            cols = slice(k * GW, (k + 1) * GW)
            upper, lower = both[:128, cols], both[128:, cols]
            value = off[:, cols] + jnp.where(lane > row, upper, lower)
            value = value + jnp.where(lane == row, diag, 0.0)
            for k_out in range(NX * NC):
                outs[k_out][q + k] = value[k_out * 16 : (k_out + 1) * 16]


def finish_kernel(tile_side, device_ref, owner_ref, *refs):
    ins, out_ref, tile_ref = refs[:8], refs[8], refs[9]
    x, core, _ = here(device_ref[0])
    tile = owner_ref[device_ref[0]]
    tile_row, tile_col = lax.div(tile, tile_side), lax.rem(tile, tile_side)
    k = 0
    for flip in range(NC):
        for d in range(NX):
            source = lax.rem(x - d + NX, NX) * 2 + (core + flip) % 2
            for rc in range(16):
                start = pl.multiple_of(source * 16 + rc // 4 * GW, 16)
                tile_ref[pl.ds(start, 16), rc % 4 * GW : (rc % 4 + 1) * GW] = ins[k][
                    pl.ds(rc, 16, stride=16), :
                ]
            k += 1

    @pl.when(tile_row < tile_col)
    def _():
        out_ref[0] = tile_ref[...]

    @pl.when(tile_row > tile_col)
    def _():
        for r in range(4):
            for c in range(4):
                out_ref[0, r * GW : (r + 1) * GW, c * GW : (c + 1) * GW] = tile_ref[
                    c * GW : (c + 1) * GW, r * GW : (r + 1) * GW
                ].T

    @pl.when(tile_row == tile_col)
    def _():
        row = lax.broadcasted_iota(jnp.int32, (GW, GW), 0)
        col = lax.broadcasted_iota(jnp.int32, (GW, GW), 1)
        for r in range(4):
            for c in range(4):
                here = tile_ref[r * GW : (r + 1) * GW, c * GW : (c + 1) * GW]
                there = tile_ref[c * GW : (c + 1) * GW, r * GW : (r + 1) * GW].T
                value = here + there
                if r == c:
                    value = jnp.where(row == col, here + 1.0, value)
                out_ref[0, r * GW : (r + 1) * GW, c * GW : (c + 1) * GW] = value


VMEM = pl.BlockSpec(memory_space=pltpu.VMEM)
SMEM = pl.BlockSpec(memory_space=pltpu.SMEM)


def shape(*dims):
    return jax.ShapeDtypeStruct(dims, F32)


def cost(flops, moved):
    return pl.CostEstimate(flops=flops, bytes_accessed=moved, transcendentals=0)


def local(effects, nominal, observed, mc_variance, theta, nuisance_index, bin_counts, tile_owner):
    chan_index, bins_index = lax.axis_index("chan"), lax.axis_index("bins")
    y, z, x, core = chan_index // NZ, chan_index % NZ, bins_index // NC, bins_index % NC
    chans, bins, width = effects.shape
    tile_side = theta.shape[0] // TILE
    slot = chan_index * (NX * NC) + bins_index
    device = slot.astype(jnp.int32).reshape(1)

    tiles = QA + QB
    mine, other = pl.pallas_call(
        bins_kernel,
        grid_spec=pltpu.PrefetchScalarGridSpec(
            num_scalar_prefetch=1,
            grid=(chans,),
            in_specs=[
                pl.BlockSpec(
                    (chans, width), lambda c, d: (lax.div(d[0], NX * NC), 0), memory_space=pltpu.SMEM
                ),
                SMEM,
                VMEM,
                VMEM,
                VMEM,
                VMEM,
                pl.BlockSpec((1, bins, width), lambda c, d: (c, 0, 0)),
            ],
            out_specs=[VMEM] * 2,
            scratch_shapes=[pltpu.VMEM((8 * GW, GW), F32)] * 3 + [pltpu.VMEM((8, width), F32)],
        ),
        out_shape=[shape(NX, tiles, 8, GW)] * 2,
        compiler_params=pltpu.CompilerParams(dimension_semantics=("arbitrary",)),
        cost_estimate=cost(2 * 10**9, 12 * 10**6),
        name="bins",
    )(device, nuisance_index, bin_counts, theta.reshape(-1, GW), nominal, observed, mc_variance, effects)
    other = lax.ppermute(other, "bins", x_shift(0, 1))
    chip = [mine[d] + other[d] for d in range(NX)]
    chip[1], nuisance_index, tile_owner = lax.optimization_barrier((chip[1], nuisance_index, tile_owner))
    arrived = [lax.ppermute(chip[d], "bins", x_shift(d, 0)) for d in (1, 2, 3)]
    own_a = chip[0][:QA] + arrived[0][:QA] + arrived[1][:QA] + arrived[2][:QA]
    own_b = chip[0][QA:] + arrived[0][QA:] + arrived[1][QA:] + arrived[2][QA:]

    at_a, at_b = gather_a(own_a), gather_b(own_b)
    order = [(dy, dz) for dy in range(NY) for dz in range(NZ)]
    arrays, offsets_a, offsets_b = [], [], []
    for at, offsets in ((at_a, offsets_a), (at_b, offsets_b)):
        for key in order:
            array, offset = at[key]
            known = [k for k, v in enumerate(arrays) if v is array]
            if not known:
                arrays.append(array)
                known = [len(arrays) - 1]
            offsets.append((known[0], offset))

    dy = jnp.arange(NY, dtype=jnp.int32)[:, None, None]
    dz = jnp.arange(NZ, dtype=jnp.int32)[None, :, None]
    channel = ((y - dy + NY) % NY * NZ + (z - dz + NZ) % NZ) * chans
    channel = (channel + jnp.arange(chans, dtype=jnp.int32)).reshape(-1)
    at = jnp.arange(channel.shape[0], dtype=jnp.int32)[:, None] == channel[None, :]
    first, second = [
        jnp.sum(jnp.where(at, nuisance_index[:, k * GW : k * GW + 1] // GW, 0), axis=0) for k in range(2)
    ]
    row_tiles = lax.dynamic_slice_in_dim(tile_owner, chan_index * 8, 8, 0)
    rel = (jnp.arange(8, dtype=jnp.int32) // NC - x + NX) % NX * NC + (jnp.arange(8, dtype=jnp.int32) + core) % NC
    per = TILE // GW

    def slot_of(tile_ids, inside):
        hit = row_tiles[:, None] == tile_ids[None, :]
        base = jnp.sum(jnp.where(hit, rel[:, None] * 16 + inside[None, :] + 1, 0), axis=0)
        return base - 1

    tr, tc = first // per, second // per
    inside = first % per * per + second % per
    straight = slot_of(tr * tile_side + tc, inside)
    mirrored = jnp.where(tr == tc, -1, slot_of(tc * tile_side + tr, inside))
    upper = slot_of(tr * (tile_side + 1), first % per * (per + 1))
    lower = slot_of(tc * (tile_side + 1), second % per * (per + 1))
    meta = jnp.stack(
        [straight, mirrored, upper, lower, first - 2 * chan_index, second - 2 * chan_index, upper, lower]
    )

    *dense, grad_rows = pl.pallas_call(
        functools.partial(place_kernel, len(arrays), offsets_a, offsets_b),
        out_shape=[shape(16, 16, GW)] * 8 + [shape(8, GW)],
        in_specs=[SMEM, VMEM] + [VMEM] * len(arrays),
        out_specs=[VMEM] * 9,
        cost_estimate=cost(10**9, 6 * 10**6),
        name="place",
    )(device, meta, *arrays)

    hops = {}
    for d in (2, 1, 3, 0):
        for flip in range(NC):
            v = dense[NC * d + flip]
            hops[flip, d] = lax.ppermute(v, "bins", x_shift(d, flip)) if d + flip else v
    ins = [hops[flip, d] for flip in range(NC) for d in range(NX)]
    hessian_tiles = pl.pallas_call(
        functools.partial(finish_kernel, tile_side),
        out_shape=shape(1, TILE, TILE),
        in_specs=[SMEM] * 2 + [VMEM] * 8,
        out_specs=VMEM,
        scratch_shapes=[pltpu.VMEM((TILE, TILE), F32)],
        cost_estimate=cost(10**6, 2 * 10**6),
        name="finish",
    )(device, tile_owner, *[v.reshape(256, GW) for v in ins])

    part = lax.dynamic_slice(
        grad_rows, (bins_index // 4, bins_index % 4 * 32), (1, 32)
    ).reshape(-1)
    gradient = part + lax.dynamic_slice_in_dim(theta, slot * 32, 32, 0)
    return hessian_tiles, gradient


def solution(mesh):
    return jax.shard_map(
        local,
        mesh=mesh,
        in_specs=(
            P("chan", "bins", None),
            P("chan", "bins"),
            P("chan", "bins"),
            P("chan", "bins"),
            P(),
            P(),
            P("chan"),
            P(),
        ),
        out_specs=(P(("chan", "bins"), None, None), P(("chan", "bins"))),
        check_vma=False,
    )
```

```python
import functools

import jax
import jax.numpy as jnp
from jax import lax
from jax.experimental import pallas as pl
from jax.experimental.pallas import tpu as pltpu
from jax.sharding import PartitionSpec as P

GW = 128
TILE = 512
NY, NZ, NX, NC = 4, 8, 4, 2
QA, QB = 18, 17
F32, BF16 = jnp.float32, jnp.bfloat16


def z_shift(s):
    return [(y * NZ + z, y * NZ + (z + s) % NZ) for y in range(NY) for z in range(NZ)]


def y_shift(s):
    return [(y * NZ + z, (y + s) % NY * NZ + z) for y in range(NY) for z in range(NZ)]


def x_shift(s, flip):
    return [(x * NC + c, (x + s) % NX * NC + (c ^ flip)) for x in range(NX) for c in range(NC)]


def on_chan(value, perm):
    return lax.ppermute(value, "chan", perm)


def gather_a(own):
    near = [own] + [on_chan(own, y_shift(d)) for d in (1, 2, 3)]
    held = jnp.concatenate(near, axis=0)
    up, down = held, held
    found = {0: held}
    for s in (1, 2, 3):
        up, down = on_chan(up, z_shift(1)), on_chan(down, z_shift(-1))
        found[s], found[NZ - s] = up, down
    half = NY // 2
    far = (on_chan(up[: half * QA], z_shift(1)), on_chan(down[half * QA :], z_shift(-1)))
    where = {(dy, dz): (found[dz], dy * QA) for dy in range(NY) for dz in range(NZ) if dz != 4}
    where.update({(dy, 4): (far[dy // half], dy % half * QA) for dy in range(NY)})
    return where


def gather_b(own):
    near = {0: own}
    for d in (1, 2, -2, -1):
        near[d % NZ] = on_chan(own, z_shift(d))
    near[3] = on_chan(near[2], z_shift(1))
    near[4] = on_chan(near[2], z_shift(2))
    near[5] = on_chan(near[6], z_shift(-1))
    held = jnp.concatenate([near[d] for d in range(NZ)], axis=0)
    up, down = on_chan(held, y_shift(1)), on_chan(held, y_shift(-1))
    half = NZ // 2
    far = (on_chan(up[: half * QB], y_shift(1)), on_chan(down[half * QB :], y_shift(-1)))
    found = {0: held, 1: up, 3: down}
    where = {(dy, dz): (found[dy], dz * QB) for dy in (0, 1, 3) for dz in range(NZ)}
    where.update({(2, dz): (far[dz // half], dz % half * QB) for dz in range(NZ)})
    return where


def here(device):
    bins_index = lax.rem(device, NX * NC)
    return lax.div(bins_index, NC), lax.rem(bins_index, NC), bins_index


def bins_kernel(
    device_ref, index_ref, counts_ref, theta_ref, nominal_ref, observed_ref, variance_ref, effects_ref,
    mine_ref, other_ref, o_ref, p_ref, d_ref, g_ref,
):
    step = pl.program_id(0)
    x, core, bins_index = here(device_ref[0])
    count = effects_ref.shape[1]
    for part in range(effects_ref.shape[0]):
        c = effects_ref.shape[0] * step + part
        effects = effects_ref[part]
        chosen = jnp.concatenate(
            [theta_ref[pl.ds(lax.div(index_ref[c, k * GW], GW), 1), :] for k in range(2)], axis=1
        )
        chosen = jnp.broadcast_to(chosen, (8, 2 * GW)).astype(BF16)
        across = effects.T
        exponent = jnp.dot(chosen, across, preferred_element_type=F32)[:1]
        expected = nominal_ref[pl.ds(c, 1), :] * jnp.exp(exponent)
        denominator = 1.0 + expected * variance_ref[pl.ds(c, 1), :]
        positions = bins_index * count + lax.broadcasted_iota(jnp.int32, (1, count), 1)
        live = positions < counts_ref[c]
        residual = jnp.where(
            live, (expected - observed_ref[pl.ds(c, 1), :].astype(F32)) / denominator, 0.0
        )
        root = jnp.sqrt(jnp.where(live, expected / denominator, 0.0))
        g_ref[pl.ds(c, 1), :] = jnp.dot(
            jnp.broadcast_to(residual, (8, count)).astype(BF16), effects, preferred_element_type=F32
        )[:1]
        scaled = (root * across.astype(F32)).astype(BF16)
        left, right = scaled[:GW], scaled[GW:]
        along = (((1,), (1,)), ((), ()))
        both = lax.dot_general(left, scaled, along, preferred_element_type=F32)
        corner = lax.dot_general(right, right, along, preferred_element_type=F32)
        row = lax.broadcasted_iota(jnp.int32, (GW, GW), 0)
        lane = lax.broadcasted_iota(jnp.int32, (GW, GW), 1)
        o_ref[part] = both[:, GW:]
        p_ref[part] = jnp.where(lane > row, both[:, :GW], corner)
        d_ref[pl.ds(c, 1), :] = jnp.sum(jnp.where(lane == row, both[:, :GW], 0.0), axis=0, keepdims=True)
        for d in range(NX):
            for ref, side in ((mine_ref, core), (other_ref, 1 - core)):
                rows = pl.ds(pl.multiple_of(lax.rem(x + d, NX) * 32 + side * 16, 16), 16)
                tile = d * (QA + QB)
                ref[pl.ds(tile * 8 + c, 16, stride=8), :] = o_ref[part, rows, :]
                ref[pl.ds((tile + QA) * 8 + c, 16, stride=8), :] = p_ref[part, rows, :]

    @pl.when(step == pl.num_programs(0) - 1)
    def _():
        for d in range(NX):
            tile = d * (QA + QB)
            for ref in (mine_ref, other_ref):
                ref[(tile + 16) * 8 : (tile + 17) * 8, :] = g_ref[:, :GW]
                ref[(tile + 17) * 8 : (tile + 18) * 8, :] = g_ref[:, GW:]
                ref[(tile + QA + 16) * 8 : (tile + QA + 17) * 8, :] = d_ref[...]


def split2(v):
    high = v.astype(BF16)
    return high, (v - high.astype(F32)).astype(BF16)


def place_kernel(arrays, offsets_a, offsets_b, device_ref, meta_ref, *refs):
    ins, outs, grad_ref = refs[:arrays], refs[arrays:-1], refs[-1]
    slice_index = here(device_ref[0])[2]
    pos = lax.broadcasted_iota(jnp.int32, (128, 256), 0)
    meta = meta_ref[...]

    def hot(*rows):
        hit = pos == meta[rows[0] : rows[0] + 1]
        for r in rows[1:]:
            hit = jnp.logical_or(hit, pos == meta[r : r + 1])
        return jnp.where(hit, 1.0, 0.0).astype(BF16)

    sel_off = hot(0, 1)
    sel_both = jnp.concatenate([hot(2), hot(3)], axis=0)
    lane = lax.broadcasted_iota(jnp.int32, (128, GW), 1)

    def gathered(offsets, q):
        return jnp.concatenate([ins[k][o + q] for k, o in offsets], axis=0)

    def apply(sel, v):
        high, low = split2(v)
        return jnp.dot(sel, high, preferred_element_type=F32) + jnp.dot(
            sel, low, preferred_element_type=F32
        )

    diag = apply(sel_both[:128], gathered(offsets_b, 16))
    grads = apply(hot(4)[:8], gathered(offsets_a, 16)) + apply(hot(5)[:8], gathered(offsets_a, 17))
    grad_ref[...] = grads
    for q in range(0, 16, 2):
        off = apply(
            sel_off, jnp.concatenate([gathered(offsets_a, q), gathered(offsets_a, q + 1)], axis=1)
        )
        both = apply(
            sel_both, jnp.concatenate([gathered(offsets_b, q), gathered(offsets_b, q + 1)], axis=1)
        )
        for k in range(2):
            row = slice_index * 16 + q + k
            cols = slice(k * GW, (k + 1) * GW)
            upper, lower = both[:128, cols], both[128:, cols]
            value = off[:, cols] + jnp.where(lane > row, upper, lower)
            value = value + jnp.where(lane == row, diag, 0.0)
            for k_out in range(NX * NC):
                outs[k_out][q + k] = value[k_out * 16 : (k_out + 1) * 16]


def finish_kernel(tile_side, device_ref, owner_ref, *refs):
    ins, out_ref, tile_ref = refs[:8], refs[8], refs[9]
    x, core, _ = here(device_ref[0])
    tile = owner_ref[device_ref[0]]
    tile_row, tile_col = lax.div(tile, tile_side), lax.rem(tile, tile_side)
    k = 0
    for flip in range(NC):
        for d in range(NX):
            source = lax.rem(x - d + NX, NX) * 2 + (core + flip) % 2
            for rc in range(16):
                start = pl.multiple_of(source * 16 + rc // 4 * GW, 16)
                tile_ref[pl.ds(start, 16), rc % 4 * GW : (rc % 4 + 1) * GW] = ins[k][
                    pl.ds(rc, 16, stride=16), :
                ]
            k += 1

    @pl.when(tile_row < tile_col)
    def _():
        out_ref[0] = tile_ref[...]

    @pl.when(tile_row > tile_col)
    def _():
        for r in range(4):
            for c in range(4):
                out_ref[0, r * GW : (r + 1) * GW, c * GW : (c + 1) * GW] = tile_ref[
                    c * GW : (c + 1) * GW, r * GW : (r + 1) * GW
                ].T

    @pl.when(tile_row == tile_col)
    def _():
        row = lax.broadcasted_iota(jnp.int32, (GW, GW), 0)
        col = lax.broadcasted_iota(jnp.int32, (GW, GW), 1)
        for r in range(4):
            for c in range(4):
                here = tile_ref[r * GW : (r + 1) * GW, c * GW : (c + 1) * GW]
                there = tile_ref[c * GW : (c + 1) * GW, r * GW : (r + 1) * GW].T
                value = here + there
                if r == c:
                    value = jnp.where(row == col, here + 1.0, value)
                out_ref[0, r * GW : (r + 1) * GW, c * GW : (c + 1) * GW] = value


VMEM = pl.BlockSpec(memory_space=pltpu.VMEM)
SMEM = pl.BlockSpec(memory_space=pltpu.SMEM)


def shape(*dims):
    return jax.ShapeDtypeStruct(dims, F32)


def cost(flops, moved):
    return pl.CostEstimate(flops=flops, bytes_accessed=moved, transcendentals=0)


def local(effects, nominal, observed, mc_variance, theta, nuisance_index, bin_counts, tile_owner):
    chan_index, bins_index = lax.axis_index("chan"), lax.axis_index("bins")
    y, z, x, core = chan_index // NZ, chan_index % NZ, bins_index // NC, bins_index % NC
    chans, bins, width = effects.shape
    tile_side = theta.shape[0] // TILE
    slot = chan_index * (NX * NC) + bins_index
    device = slot.astype(jnp.int32).reshape(1)

    tiles = QA + QB
    mine, other = pl.pallas_call(
        bins_kernel,
        grid_spec=pltpu.PrefetchScalarGridSpec(
            num_scalar_prefetch=1,
            grid=(chans // 2,),
            in_specs=[
                pl.BlockSpec(
                    (chans, width), lambda c, d: (lax.div(d[0], NX * NC), 0), memory_space=pltpu.SMEM
                ),
                SMEM,
                VMEM,
                VMEM,
                VMEM,
                VMEM,
                pl.BlockSpec((2, bins, width), lambda c, d: (c, 0, 0)),
            ],
            out_specs=[VMEM] * 2,
            scratch_shapes=[pltpu.VMEM((2, GW, GW), F32)] * 2
            + [pltpu.VMEM((8, GW), F32), pltpu.VMEM((8, width), F32)],
        ),
        out_shape=[shape(NX * tiles * 8, GW)] * 2,
        compiler_params=pltpu.CompilerParams(dimension_semantics=("arbitrary",)),
        cost_estimate=cost(2 * 10**9, 12 * 10**6),
        name="bins",
    )(device, nuisance_index, bin_counts, theta.reshape(-1, GW), nominal, observed, mc_variance, effects)
    mine, other = [v.reshape(NX, tiles, 8, GW) for v in (mine, other)]
    other = lax.ppermute(other, "bins", x_shift(0, 1))
    chip = [mine[d] + other[d] for d in range(NX)]
    chip[1], nuisance_index, tile_owner = lax.optimization_barrier((chip[1], nuisance_index, tile_owner))
    arrived = [lax.ppermute(chip[d], "bins", x_shift(d, 0)) for d in (1, 2, 3)]
    own_a = chip[0][:QA] + arrived[0][:QA] + arrived[1][:QA] + arrived[2][:QA]
    own_b = chip[0][QA:] + arrived[0][QA:] + arrived[1][QA:] + arrived[2][QA:]

    at_a, at_b = gather_a(own_a), gather_b(own_b)
    order = [(dy, dz) for dy in range(NY) for dz in range(NZ)]
    arrays, offsets_a, offsets_b = [], [], []
    for at, offsets in ((at_a, offsets_a), (at_b, offsets_b)):
        for key in order:
            array, offset = at[key]
            known = [k for k, v in enumerate(arrays) if v is array]
            if not known:
                arrays.append(array)
                known = [len(arrays) - 1]
            offsets.append((known[0], offset))

    dy = jnp.arange(NY, dtype=jnp.int32)[:, None, None]
    dz = jnp.arange(NZ, dtype=jnp.int32)[None, :, None]
    channel = ((y - dy + NY) % NY * NZ + (z - dz + NZ) % NZ) * chans
    channel = (channel + jnp.arange(chans, dtype=jnp.int32)).reshape(-1)
    at = jnp.arange(channel.shape[0], dtype=jnp.int32)[:, None] == channel[None, :]
    first, second = [
        jnp.sum(jnp.where(at, nuisance_index[:, k * GW : k * GW + 1] // GW, 0), axis=0) for k in range(2)
    ]
    row_tiles = lax.dynamic_slice_in_dim(tile_owner, chan_index * 8, 8, 0)
    rel = (jnp.arange(8, dtype=jnp.int32) // NC - x + NX) % NX * NC + (jnp.arange(8, dtype=jnp.int32) + core) % NC
    per = TILE // GW

    def slot_of(tile_ids, inside):
        hit = row_tiles[:, None] == tile_ids[None, :]
        base = jnp.sum(jnp.where(hit, rel[:, None] * 16 + inside[None, :] + 1, 0), axis=0)
        return base - 1

    tr, tc = first // per, second // per
    inside = first % per * per + second % per
    straight = slot_of(tr * tile_side + tc, inside)
    mirrored = jnp.where(tr == tc, -1, slot_of(tc * tile_side + tr, inside))
    upper = slot_of(tr * (tile_side + 1), first % per * (per + 1))
    lower = slot_of(tc * (tile_side + 1), second % per * (per + 1))
    meta = jnp.stack(
        [straight, mirrored, upper, lower, first - 2 * chan_index, second - 2 * chan_index, upper, lower]
    )

    *dense, grad_rows = pl.pallas_call(
        functools.partial(place_kernel, len(arrays), offsets_a, offsets_b),
        out_shape=[shape(16, 16, GW)] * 8 + [shape(8, GW)],
        in_specs=[SMEM, VMEM] + [VMEM] * len(arrays),
        out_specs=[VMEM] * 9,
        cost_estimate=cost(10**9, 6 * 10**6),
        name="place",
    )(device, meta, *arrays)

    hops = {}
    for d in (2, 1, 3, 0):
        for flip in range(NC):
            v = dense[NC * d + flip]
            hops[flip, d] = lax.ppermute(v, "bins", x_shift(d, flip)) if d + flip else v
    ins = [hops[flip, d] for flip in range(NC) for d in range(NX)]
    hessian_tiles = pl.pallas_call(
        functools.partial(finish_kernel, tile_side),
        out_shape=shape(1, TILE, TILE),
        in_specs=[SMEM] * 2 + [VMEM] * 8,
        out_specs=VMEM,
        scratch_shapes=[pltpu.VMEM((TILE, TILE), F32)],
        cost_estimate=cost(10**6, 2 * 10**6),
        name="finish",
    )(device, tile_owner, *[v.reshape(256, GW) for v in ins])

    part = lax.dynamic_slice(
        grad_rows, (bins_index // 4, bins_index % 4 * 32), (1, 32)
    ).reshape(-1)
    gradient = part + lax.dynamic_slice_in_dim(theta, slot * 32, 32, 0)
    return hessian_tiles, gradient


def solution(mesh):
    return jax.shard_map(
        local,
        mesh=mesh,
        in_specs=(
            P("chan", "bins", None),
            P("chan", "bins"),
            P("chan", "bins"),
            P("chan", "bins"),
            P(),
            P(),
            P("chan"),
            P(),
        ),
        out_specs=(P(("chan", "bins"), None, None), P(("chan", "bins"))),
        check_vma=False,
    )
```

```python
import functools

import jax
import jax.numpy as jnp
from jax import lax
from jax.experimental import pallas as pl
from jax.experimental.pallas import tpu as pltpu
from jax.sharding import PartitionSpec as P

GW = 128
TILE = 512
NY, NZ, NX, NC = 4, 8, 4, 2
QA, QB = 18, 17
F32, BF16 = jnp.float32, jnp.bfloat16


def z_shift(s):
    return [(y * NZ + z, y * NZ + (z + s) % NZ) for y in range(NY) for z in range(NZ)]


def y_shift(s):
    return [(y * NZ + z, (y + s) % NY * NZ + z) for y in range(NY) for z in range(NZ)]


def x_shift(s, flip):
    return [(x * NC + c, (x + s) % NX * NC + (c ^ flip)) for x in range(NX) for c in range(NC)]


def on_chan(value, perm):
    return lax.ppermute(value, "chan", perm)


def gather_a(own):
    near = [own] + [on_chan(own, y_shift(d)) for d in (1, 2, 3)]
    held = jnp.concatenate(near, axis=0)
    up, down = held, held
    found = {0: held}
    for s in (1, 2, 3):
        up, down = on_chan(up, z_shift(1)), on_chan(down, z_shift(-1))
        found[s], found[NZ - s] = up, down
    half = NY // 2
    far = (on_chan(up[: half * QA], z_shift(1)), on_chan(down[half * QA :], z_shift(-1)))
    where = {(dy, dz): (found[dz], dy * QA) for dy in range(NY) for dz in range(NZ) if dz != 4}
    where.update({(dy, 4): (far[dy // half], dy % half * QA) for dy in range(NY)})
    return where


def gather_b(own):
    near = {0: own}
    for d in (1, 2, -2, -1):
        near[d % NZ] = on_chan(own, z_shift(d))
    near[3] = on_chan(near[2], z_shift(1))
    near[4] = on_chan(near[2], z_shift(2))
    near[5] = on_chan(near[6], z_shift(-1))
    held = jnp.concatenate([near[d] for d in range(NZ)], axis=0)
    up, down = on_chan(held, y_shift(1)), on_chan(held, y_shift(-1))
    half = NZ // 2
    far = (on_chan(up[: half * QB], y_shift(1)), on_chan(down[half * QB :], y_shift(-1)))
    found = {0: held, 1: up, 3: down}
    where = {(dy, dz): (found[dy], dz * QB) for dy in (0, 1, 3) for dz in range(NZ)}
    where.update({(2, dz): (far[dz // half], dz % half * QB) for dz in range(NZ)})
    return where


def here(device):
    bins_index = lax.rem(device, NX * NC)
    return lax.div(bins_index, NC), lax.rem(bins_index, NC), bins_index


def bins_kernel(
    device_ref, index_ref, counts_ref, theta_ref, nominal_ref, observed_ref, variance_ref, effects_ref,
    mine_ref, other_ref, o_ref, p_ref, d_ref, g_ref,
):
    step = pl.program_id(0)
    x, core, bins_index = here(device_ref[0])
    count = effects_ref.shape[1]
    for part in range(effects_ref.shape[0]):
        c = effects_ref.shape[0] * step + part
        effects = effects_ref[part]
        chosen = jnp.concatenate(
            [theta_ref[pl.ds(lax.div(index_ref[c, k * GW], GW), 1), :] for k in range(2)], axis=1
        )
        chosen = jnp.broadcast_to(chosen, (8, 2 * GW)).astype(BF16)
        across = effects.T
        exponent = jnp.dot(chosen, across, preferred_element_type=F32)[:1]
        expected = nominal_ref[pl.ds(c, 1), :] * jnp.exp(exponent)
        denominator = 1.0 + expected * variance_ref[pl.ds(c, 1), :]
        positions = bins_index * count + lax.broadcasted_iota(jnp.int32, (1, count), 1)
        live = positions < counts_ref[c]
        residual = jnp.where(
            live, (expected - observed_ref[pl.ds(c, 1), :].astype(F32)) / denominator, 0.0
        )
        root = jnp.sqrt(jnp.where(live, expected / denominator, 0.0))
        g_ref[pl.ds(c, 1), :] = jnp.dot(
            jnp.broadcast_to(residual, (8, count)).astype(BF16), effects, preferred_element_type=F32
        )[:1]
        scaled = (root * across.astype(F32)).astype(BF16)
        left, right = scaled[:GW], scaled[GW:]
        along = (((1,), (1,)), ((), ()))
        both = lax.dot_general(left, scaled, along, preferred_element_type=F32)
        corner = lax.dot_general(right, right, along, preferred_element_type=F32)
        row = lax.broadcasted_iota(jnp.int32, (GW, GW), 0)
        lane = lax.broadcasted_iota(jnp.int32, (GW, GW), 1)
        o_ref[part] = both[:, GW:]
        p_ref[part] = jnp.where(lane > row, both[:, :GW], corner)
        d_ref[pl.ds(c, 1), :] = jnp.sum(jnp.where(lane == row, both[:, :GW], 0.0), axis=0, keepdims=True)
        for d in range(NX):
            for ref, side in ((mine_ref, core), (other_ref, 1 - core)):
                rows = pl.ds(pl.multiple_of(lax.rem(x + d, NX) * 32 + side * 16, 16), 16)
                tile = d * (QA + QB)
                ref[pl.ds(tile * 8 + c, 16, stride=8), :] = o_ref[part, rows, :]
                ref[pl.ds((tile + QA) * 8 + c, 16, stride=8), :] = p_ref[part, rows, :]

    @pl.when(step == pl.num_programs(0) - 1)
    def _():
        for d in range(NX):
            tile = d * (QA + QB)
            for ref in (mine_ref, other_ref):
                ref[(tile + 16) * 8 : (tile + 17) * 8, :] = g_ref[:, :GW]
                ref[(tile + 17) * 8 : (tile + 18) * 8, :] = g_ref[:, GW:]
                ref[(tile + QA + 16) * 8 : (tile + QA + 17) * 8, :] = d_ref[...]


def split2(v):
    high = v.astype(BF16)
    return high, (v - high.astype(F32)).astype(BF16)


def place_kernel(arrays, offsets_a, offsets_b, device_ref, meta_ref, *refs):
    ins, outs, grad_ref = refs[:arrays], refs[arrays:-1], refs[-1]
    slice_index = here(device_ref[0])[2]
    pos = lax.broadcasted_iota(jnp.int32, (128, 256), 0)
    meta = meta_ref[...]

    def hot(*rows):
        hit = pos == meta[rows[0] : rows[0] + 1]
        for r in rows[1:]:
            hit = jnp.logical_or(hit, pos == meta[r : r + 1])
        return jnp.where(hit, 1.0, 0.0).astype(BF16)

    sel_off = hot(0, 1)
    sel_both = jnp.concatenate([hot(2), hot(3)], axis=0)
    lane = lax.broadcasted_iota(jnp.int32, (128, GW), 1)

    def gathered(offsets, q):
        return jnp.concatenate([ins[k][o + q] for k, o in offsets], axis=0)

    def apply(sel, v):
        high, low = split2(v)
        return jnp.dot(sel, high, preferred_element_type=F32) + jnp.dot(
            sel, low, preferred_element_type=F32
        )

    diag = apply(sel_both[:128], gathered(offsets_b, 16))
    grads = apply(hot(4)[:8], gathered(offsets_a, 16)) + apply(hot(5)[:8], gathered(offsets_a, 17))
    grad_ref[...] = grads
    for q in range(0, 16, 2):
        off = apply(
            sel_off, jnp.concatenate([gathered(offsets_a, q), gathered(offsets_a, q + 1)], axis=1)
        )
        both = apply(
            sel_both, jnp.concatenate([gathered(offsets_b, q), gathered(offsets_b, q + 1)], axis=1)
        )
        for k in range(2):
            row = slice_index * 16 + q + k
            cols = slice(k * GW, (k + 1) * GW)
            upper, lower = both[:128, cols], both[128:, cols]
            value = off[:, cols] + jnp.where(lane > row, upper, lower)
            value = value + jnp.where(lane == row, diag, 0.0)
            for k_out in range(NX * NC):
                outs[k_out][q + k] = value[k_out * 16 : (k_out + 1) * 16]


def finish_kernel(tile_side, device_ref, owner_ref, *refs):
    ins, out_ref, tile_ref = refs[:8], refs[8], refs[9]
    x, core, _ = here(device_ref[0])
    tile = owner_ref[device_ref[0]]
    tile_row, tile_col = lax.div(tile, tile_side), lax.rem(tile, tile_side)
    k = 0
    for flip in range(NC):
        for d in range(NX):
            source = lax.rem(x - d + NX, NX) * 2 + (core + flip) % 2
            for rc in range(16):
                start = pl.multiple_of(source * 16 + rc // 4 * GW, 16)
                tile_ref[pl.ds(start, 16), rc % 4 * GW : (rc % 4 + 1) * GW] = ins[k][
                    pl.ds(rc, 16, stride=16), :
                ]
            k += 1

    @pl.when(tile_row < tile_col)
    def _():
        out_ref[0] = tile_ref[...]

    @pl.when(tile_row > tile_col)
    def _():
        for r in range(4):
            for c in range(4):
                out_ref[0, r * GW : (r + 1) * GW, c * GW : (c + 1) * GW] = tile_ref[
                    c * GW : (c + 1) * GW, r * GW : (r + 1) * GW
                ].T

    @pl.when(tile_row == tile_col)
    def _():
        row = lax.broadcasted_iota(jnp.int32, (GW, GW), 0)
        col = lax.broadcasted_iota(jnp.int32, (GW, GW), 1)
        for r in range(4):
            for c in range(4):
                here = tile_ref[r * GW : (r + 1) * GW, c * GW : (c + 1) * GW]
                there = tile_ref[c * GW : (c + 1) * GW, r * GW : (r + 1) * GW].T
                value = here + there
                if r == c:
                    value = jnp.where(row == col, here + 1.0, value)
                out_ref[0, r * GW : (r + 1) * GW, c * GW : (c + 1) * GW] = value


VMEM = pl.BlockSpec(memory_space=pltpu.VMEM)
SMEM = pl.BlockSpec(memory_space=pltpu.SMEM)


def shape(*dims):
    return jax.ShapeDtypeStruct(dims, F32)


def cost(flops, moved):
    return pl.CostEstimate(flops=flops, bytes_accessed=moved, transcendentals=0)


def local(effects, nominal, observed, mc_variance, theta, nuisance_index, bin_counts, tile_owner):
    chan_index, bins_index = lax.axis_index("chan"), lax.axis_index("bins")
    y, z, x, core = chan_index // NZ, chan_index % NZ, bins_index // NC, bins_index % NC
    chans, bins, width = effects.shape
    tile_side = theta.shape[0] // TILE
    slot = chan_index * (NX * NC) + bins_index
    device = slot.astype(jnp.int32).reshape(1)

    tiles = QA + QB
    mine, other = pl.pallas_call(
        bins_kernel,
        grid_spec=pltpu.PrefetchScalarGridSpec(
            num_scalar_prefetch=1,
            grid=(chans // 2,),
            in_specs=[
                pl.BlockSpec(
                    (chans, width), lambda c, d: (lax.div(d[0], NX * NC), 0), memory_space=pltpu.SMEM
                ),
                SMEM,
                VMEM,
                VMEM,
                VMEM,
                VMEM,
                pl.BlockSpec((2, bins, width), lambda c, d: (c, 0, 0)),
            ],
            out_specs=[VMEM] * 2,
            scratch_shapes=[pltpu.VMEM((2, GW, GW), F32)] * 2
            + [pltpu.VMEM((8, GW), F32), pltpu.VMEM((8, width), F32)],
        ),
        out_shape=[shape(NX * tiles * 8, GW)] * 2,
        compiler_params=pltpu.CompilerParams(dimension_semantics=("arbitrary",)),
        cost_estimate=cost(2 * 10**9, 12 * 10**6),
        name="bins",
    )(device, nuisance_index, bin_counts, theta.reshape(-1, GW), nominal, observed, mc_variance, effects)
    mine, other = [v.reshape(NX, tiles, 8, GW) for v in (mine, other)]
    other = lax.ppermute(other, "bins", x_shift(0, 1))
    chip = [mine[d] + other[d] for d in range(NX)]
    chip[1], nuisance_index, tile_owner = lax.optimization_barrier((chip[1], nuisance_index, tile_owner))
    arrived = [lax.ppermute(chip[d], "bins", x_shift(d, 0)) for d in (1, 2, 3)]
    own_a = chip[0][:QA] + arrived[0][:QA] + arrived[1][:QA] + arrived[2][:QA]
    own_b = chip[0][QA:] + arrived[0][QA:] + arrived[1][QA:] + arrived[2][QA:]

    at_a, at_b = gather_a(own_a), gather_b(own_b)
    order = [(dy, dz) for dy in range(NY) for dz in range(NZ)]
    arrays, offsets_a, offsets_b = [], [], []
    for at, offsets in ((at_a, offsets_a), (at_b, offsets_b)):
        for key in order:
            array, offset = at[key]
            known = [k for k, v in enumerate(arrays) if v is array]
            if not known:
                arrays.append(array)
                known = [len(arrays) - 1]
            offsets.append((known[0], offset))

    dy = jnp.arange(NY, dtype=jnp.int32)[:, None, None]
    dz = jnp.arange(NZ, dtype=jnp.int32)[None, :, None]
    channel = ((y - dy + NY) % NY * NZ + (z - dz + NZ) % NZ) * chans
    channel = (channel + jnp.arange(chans, dtype=jnp.int32)).reshape(-1)
    at = jnp.arange(channel.shape[0], dtype=jnp.int32)[:, None] == channel[None, :]
    first, second = [
        jnp.sum(jnp.where(at, nuisance_index[:, k * GW : k * GW + 1] // GW, 0), axis=0) for k in range(2)
    ]
    row_tiles = lax.dynamic_slice_in_dim(tile_owner, chan_index * 8, 8, 0)
    rel = (jnp.arange(8, dtype=jnp.int32) // NC - x + NX) % NX * NC + (jnp.arange(8, dtype=jnp.int32) + core) % NC
    per = TILE // GW

    def slot_of(tile_ids, inside):
        hit = row_tiles[:, None] == tile_ids[None, :]
        base = jnp.sum(jnp.where(hit, rel[:, None] * 16 + inside[None, :] + 1, 0), axis=0)
        return base - 1

    tr, tc = first // per, second // per
    inside = first % per * per + second % per
    straight = slot_of(tr * tile_side + tc, inside)
    mirrored = jnp.where(tr == tc, -1, slot_of(tc * tile_side + tr, inside))
    upper = slot_of(tr * (tile_side + 1), first % per * (per + 1))
    lower = slot_of(tc * (tile_side + 1), second % per * (per + 1))
    meta = jnp.stack(
        [straight, mirrored, upper, lower, first - 2 * chan_index, second - 2 * chan_index, upper, lower]
    )

    *dense, grad_rows = pl.pallas_call(
        functools.partial(place_kernel, len(arrays), offsets_a, offsets_b),
        out_shape=[shape(16, 16, GW)] * 8 + [shape(8, GW)],
        in_specs=[SMEM, VMEM] + [VMEM] * len(arrays),
        out_specs=[VMEM] * 9,
        cost_estimate=cost(10**9, 6 * 10**6),
        compiler_params=pltpu.CompilerParams(vmem_limit_bytes=24 * 2**20),
        name="place",
    )(device, meta, *arrays)

    hops = {}
    for d in (2, 1, 3, 0):
        for flip in range(NC):
            v = dense[NC * d + flip]
            hops[flip, d] = lax.ppermute(v, "bins", x_shift(d, flip)) if d + flip else v
    ins = [hops[flip, d] for flip in range(NC) for d in range(NX)]
    hessian_tiles = pl.pallas_call(
        functools.partial(finish_kernel, tile_side),
        out_shape=shape(1, TILE, TILE),
        in_specs=[SMEM] * 2 + [VMEM] * 8,
        out_specs=VMEM,
        scratch_shapes=[pltpu.VMEM((TILE, TILE), F32)],
        cost_estimate=cost(10**6, 2 * 10**6),
        compiler_params=pltpu.CompilerParams(vmem_limit_bytes=12 * 2**20),
        name="finish",
    )(device, tile_owner, *[v.reshape(256, GW) for v in ins])

    part = lax.dynamic_slice(
        grad_rows, (bins_index // 4, bins_index % 4 * 32), (1, 32)
    ).reshape(-1)
    gradient = part + lax.dynamic_slice_in_dim(theta, slot * 32, 32, 0)
    return hessian_tiles, gradient


def solution(mesh):
    return jax.shard_map(
        local,
        mesh=mesh,
        in_specs=(
            P("chan", "bins", None),
            P("chan", "bins"),
            P("chan", "bins"),
            P("chan", "bins"),
            P(),
            P(),
            P("chan"),
            P(),
        ),
        out_specs=(P(("chan", "bins"), None, None), P(("chan", "bins"))),
        check_vma=False,
    )
```
